32 devices in a mesh: dp: 4 (over y, x), ctx: 8 (over z, core).
Axes of the slice: x: 2, y: 2, z: 4, core: 2. Of those that a mesh axis runs over, the one named last changes fastest.
Arguments:
- tokens: bfloat16 [4, 1024, 1536], P('dp', 'ctx'), may hold values from -6 to 6
- positions: int32 [4, 1024], P('dp', 'ctx'), may hold values from 0 to 3071, as said below
- block_order: int32 [16], replicated, may hold values from 0 to 15, as said below
- cotangent: bfloat16 [4, 1024, 1536], P('dp', 'ctx'), may hold values from -6 to 6
- gain_attn: bfloat16 [1536], P('dp'), may hold values from 0.099609375 to 1.8984375
- w_qkv: bfloat16 [1536, 2048], P('dp'), may hold values from -0.15625 to 0.15625
- b_qkv: bfloat16 [2048], P('dp'), may hold values from -3 to 3
- w_out: bfloat16 [1536, 1536], P('dp'), may hold values from -1.75 to 1.75
- gain_mlp: bfloat16 [1536], P('dp'), may hold values from 0.099609375 to 1.8984375
- w_gate: bfloat16 [1536, 8960], P('dp'), may hold values from -0.15625 to 0.15625
- w_up: bfloat16 [1536, 8960], P('dp'), may hold values from -0.15625 to 0.15625
- w_down: bfloat16 [8960, 1536], P('dp'), may hold values from -0.0625 to 0.0625
Outputs:
- block_out: bfloat16 [4, 1024, 1536], P('dp', 'ctx')
- grad_tokens: float32 [4, 1024, 1536], P('dp', 'ctx')
- grad_gain_attn: float32 [1536], P(('dp', 'ctx'))
- grad_w_qkv: float32 [1536, 2048], P(('dp', 'ctx'))
- grad_b_qkv: float32 [2048], P(('dp', 'ctx'))
- grad_w_out: float32 [1536, 1536], P(('dp', 'ctx'))
- grad_gain_mlp: float32 [1536], P(('dp', 'ctx'))
- grad_w_gate: float32 [1536, 8960], P(('dp', 'ctx'))
- grad_w_up: float32 [1536, 8960], P(('dp', 'ctx'))
- grad_w_down: float32 [8960, 1536], P(('dp', 'ctx'))
The draws below stay inside these ranges and needn't reach their ends.
Inputs may be any that keep to these rules, and one draw needn't show every extreme that they name: A permutation in which entries 2c and 2c + 1 always add up to 15; the device of index c along ctx stores, as its first and its second 64 tokens of every sequence, that sequence's sub-blocks block_order[2c] and block_order[2c + 1]. positions[s, t] is an offset of sequence s, from 0 to 2048, plus the index idx(t) of the token stored at place t; the first sequence's offset is 0 and the last one's 2 * 1024.
All inputs are finite; a program needn't handle non-finite values.
Results may differ from the reference program's by a relative error of at most 0.02.
Values may be sent and summed in bfloat16 or wider, within the bound.
No kernel may reach another device: no remote copies, remote signals or barrier semaphores. Data moves between devices by JAX's collectives and lax.ppermute only.
A program may use at most 576 MiB of HBM per device.

```python
import math
from functools import partial
import jax
import jax.numpy as jnp
from jax import lax

D = 1536
HEADS = 12
KV_HEADS = 2
HEAD_DIM = 128
FF = 8960
QKV = 2048
SEQS = 4
SEQ_LEN = 1024
SUB = 64
BLOCKS = 16


def pair_order(key):
    pair_count = BLOCKS // 2
    pair_ids = jax.random.permutation(jax.random.fold_in(key, 11), pair_count).astype(jnp.int32)
    flip_bits = jax.random.randint(jax.random.fold_in(key, 12), (pair_count,), 0, 2)
    front_half = jnp.where(flip_bits == 1, pair_ids, BLOCKS - 1 - pair_ids)
    return jnp.stack([front_half, BLOCKS - 1 - front_half], axis=1).reshape(BLOCKS).astype(jnp.int32)


def draw_block_order(key, part):
    return pair_order(key)


def draw_positions(key, part):
    block_ids = pair_order(key)
    places = jnp.arange(SEQ_LEN, dtype=jnp.int32)
    logical = block_ids[places // SUB] * SUB + places % SUB
    offsets = jax.random.randint(jax.random.fold_in(key, 13), (SEQS, 1), 0, 2 * SEQ_LEN + 1).astype(jnp.int32)
    offsets = offsets.at[0, 0].set(0).at[SEQS - 1, 0].set(2 * SEQ_LEN)
    return (offsets + logical[None, :]).astype(jnp.int32)


def block_scale(key, shape, split, smallest, top_value):
    def one(dim, shards_of):
        heights = jax.random.uniform(jax.random.fold_in(jax.random.fold_in(key, 6), dim), (shards_of,), jnp.float32, smallest / len(split), top_value / len(split))
        return jnp.repeat(jnp.exp(heights), shape[dim] // shards_of).reshape((-1,) + (1,) * (len(shape) - dim - 1))

    factor_of = one(*split[0])
    for cut in split[1:]:
        factor_of = factor_of * one(*cut)
    return factor_of


def noise(rng, extent, spread, limit, split=(), held_as=jnp.bfloat16):
    entries = spread * jax.random.normal(rng, extent, jnp.float32)
    if split:
        entries = entries * block_scale(rng, extent, split, -0.22, 0.18)
    return jnp.clip(entries, -limit, limit).astype(held_as)


def setup_inputs(seed: int = 0) -> dict:
    splits = jax.random.split(jax.random.key(seed), 13)
    tokens = noise(splits[0], (SEQS, SEQ_LEN, D), 1.0, 6.0, ((0, 4), (1, 8)))
    positions = draw_positions(jax.random.fold_in(splits[12], 71), 0)
    block_order = draw_block_order(jax.random.fold_in(splits[12], 71), 0)
    cotangent = noise(splits[3], (SEQS, SEQ_LEN, D), 1.0, 6.0, ((0, 4), (1, 8)))
    gain_attn = jnp.clip(1.0 + 0.18 * jax.random.normal(splits[4], (D,), jnp.float32), 0.099609375, 1.8984375).astype(jnp.bfloat16)
    w_qkv = noise(splits[5], (D, QKV), D ** -0.5, 0.15625, ((0, 4),))
    b_qkv = noise(splits[6], (QKV,), 0.5, 3.0, ((0, 4),))
    w_out = noise(splits[7], (D, D), (D // 128) ** -0.5, 1.75, ((0, 4),))
    gain_mlp = jnp.clip(1.0 + 0.18 * jax.random.normal(splits[8], (D,), jnp.float32), 0.099609375, 1.8984375).astype(jnp.bfloat16)
    w_gate = noise(splits[9], (D, FF), D ** -0.5, 0.15625, ((0, 4),))
    w_up = noise(splits[10], (D, FF), D ** -0.5, 0.15625, ((0, 4),))
    w_down = noise(splits[11], (FF, D), FF ** -0.5, 0.0625, ((0, 4),))
    return {"tokens": tokens, "positions": positions, "block_order": block_order, "cotangent": cotangent, "gain_attn": gain_attn, "w_qkv": w_qkv, "b_qkv": b_qkv, "w_out": w_out, "gain_mlp": gain_mlp, "w_gate": w_gate, "w_up": w_up, "w_down": w_down}


rope_base = 1000000.0
norm_eps = 1e-06
masked_score = -1e+30

@jax.custom_vjp
def low(v):
    return lax.optimization_barrier(v.astype(jnp.bfloat16)).astype(jnp.float32)

@jax.custom_vjp
def low_back(v):
    return v

def low_keep(v):
    return (low(v), None)

def low_pass(kept, grad):
    return (grad,)

def back_keep(v):
    return (v, None)

def back_low(kept, grad):
    return (low(grad),)
low.defvjp(low_keep, low_pass)
low_back.defvjp(back_keep, back_low)

def matmul(left, right):
    return jnp.dot(left, right, precision=lax.Precision.HIGHEST, preferred_element_type=jnp.float32)

def normalize(rows_in):
    return rows_in * lax.rsqrt(lax.optimization_barrier(jnp.mean(rows_in * rows_in, axis=-1, keepdims=True)) + norm_eps)

def rope_tables(token_positions, head_dim):
    half_dim = head_dim // 2
    half_steps = jnp.arange(half_dim, dtype=jnp.float32)
    frequency = jnp.exp(-math.log(rope_base) * (2.0 * half_steps / head_dim))
    angles = token_positions.astype(jnp.float32)[:, None] * frequency[None, :]
    return (jnp.cos(angles), jnp.sin(angles))

def rotate(head_rows, cosines, sines):
    half_dim = head_rows.shape[-1] // 2
    front_half = head_rows[..., :half_dim]
    back_half = head_rows[..., half_dim:]
    cosine_part = cosines[:, None, :]
    sine_part = sines[:, None, :]
    return jnp.concatenate([front_half * cosine_part - back_half * sine_part, back_half * cosine_part + front_half * sine_part], axis=-1)

def forward_sequence(cosines, sines, inputs, gain_attn, w_qkv, b_qkv, w_out, gain_mlp, w_gate, w_up, w_down):
    length = inputs.shape[0]
    groups = HEADS // KV_HEADS
    query_width = HEADS * HEAD_DIM
    kv_width = KV_HEADS * HEAD_DIM
    score_scale = 1.0 / math.sqrt(HEAD_DIM)
    hidden_one = low(normalize(inputs) * gain_attn)
    projected = low_back(matmul(hidden_one, w_qkv) + b_qkv)
    queries = low(rotate(projected[:, :query_width].reshape(length, HEADS, HEAD_DIM), cosines, sines))
    queries = queries.reshape(length, KV_HEADS, groups, HEAD_DIM)
    key_rows = low(rotate(projected[:, query_width:query_width + kv_width].reshape(length, KV_HEADS, HEAD_DIM), cosines, sines))
    value_rows = low(projected[:, query_width + kv_width:].reshape(length, KV_HEADS, HEAD_DIM))
    block_rows = min(512, length)
    key_index = jnp.arange(length, dtype=jnp.int32)

    def attend_block(start_index):
        query_block = lax.dynamic_slice_in_dim(queries, start_index, block_rows, 0)
        scores = jnp.einsum('tkgd,ukd->kgtu', query_block, key_rows, precision=lax.Precision.HIGHEST) * score_scale
        scores = low_back(scores)
        query_index = start_index + jnp.arange(block_rows, dtype=jnp.int32)
        allowed = key_index[None, :] <= query_index[:, None]
        masked = jnp.where(allowed, scores, masked_score)
        row_max = lax.optimization_barrier(jnp.max(masked, axis=-1, keepdims=True))
        log_total = row_max + jnp.log(lax.optimization_barrier(jnp.sum(jnp.exp(masked - row_max), axis=-1, keepdims=True)))
        probs_full = low(jnp.where(allowed, jnp.exp(masked - log_total), 0.0))
        block_out = jnp.einsum('kgtu,ukd->tkgd', probs_full, value_rows, precision=lax.Precision.HIGHEST)
        return block_out.reshape(block_rows, query_width)
    start_list = jnp.arange(length // block_rows, dtype=jnp.int32) * block_rows
    attended = lax.map(jax.checkpoint(attend_block), start_list).reshape(length, query_width)
    attended = low_back(low(attended))
    middle = inputs + low_back(matmul(attended, w_out))
    hidden_two = low(normalize(middle) * gain_mlp)
    gate_values = low_back(matmul(hidden_two, w_gate))
    up_values = low_back(matmul(hidden_two, w_up))
    activated = low(jax.nn.silu(gate_values) * up_values)
    return middle + low_back(matmul(activated, w_down))

def reference(tokens, positions, block_order, cotangent, gain_attn, w_qkv, b_qkv, w_out, gain_mlp, w_gate, w_up, w_down):
    places = jnp.arange(SEQ_LEN, dtype=jnp.int32)
    slot_of_block = jnp.zeros((BLOCKS,), jnp.int32).at[block_order.astype(jnp.int32)].set(jnp.arange(BLOCKS, dtype=jnp.int32))
    from_store = (slot_of_block[places // SUB] * SUB + places % SUB).astype(jnp.int32)
    to_logical = (block_order.astype(jnp.int32)[places // SUB] * SUB + places % SUB).astype(jnp.int32)
    weights = (gain_attn.astype(jnp.float32), w_qkv.astype(jnp.float32), b_qkv.astype(jnp.float32), w_out.astype(jnp.float32), gain_mlp.astype(jnp.float32), w_gate.astype(jnp.float32), w_up.astype(jnp.float32), w_down.astype(jnp.float32))

    def per_sequence(totals, seq_items):
        stored_tokens, stored_positions, stored_cotangent = seq_items
        inputs = stored_tokens[from_store].astype(jnp.float32)
        cosines, sines = rope_tables(stored_positions[from_store], HEAD_DIM)
        grad_in = stored_cotangent[from_store].astype(jnp.float32)
        result, pullback = jax.vjp(partial(forward_sequence, cosines, sines), inputs, weights[0], weights[1], weights[2], weights[3], weights[4], weights[5], weights[6], weights[7])
        grad_terms = pullback(grad_in)
        totals = tuple((earlier + later for earlier, later in zip(totals, grad_terms[1:])))
        return (totals, (result[to_logical].astype(jnp.bfloat16), grad_terms[0][to_logical]))
    start_totals = tuple((jnp.zeros_like(member) for member in weights))
    totals, outputs = lax.scan(per_sequence, start_totals, (tokens, positions, cotangent))
    block_out, grad_tokens = outputs
    return (block_out, grad_tokens, totals[0], totals[1], totals[2], totals[3], totals[4], totals[5], totals[6], totals[7])
```

```python
import functools
import math

import jax
import jax.numpy as jnp
from jax import lax
from jax.experimental import pallas as pl
from jax.experimental.pallas import tpu as pltpu
from jax.sharding import PartitionSpec as P

HEADS = 12
KV_HEADS = 2
HEAD_DIM = 128
GROUPS = HEADS // KV_HEADS
QW = HEADS * HEAD_DIM
KW = KV_HEADS * HEAD_DIM
STEP_HEADS = 3

rope_base = 1000000.0
norm_eps = 1e-06
masked_score = -1e30
score_scale = 1.0 / math.sqrt(HEAD_DIM)
f32 = jnp.float32
bf16 = jnp.bfloat16


def exchange(value, axis, bit):
    count = lax.axis_size(axis)
    return lax.ppermute(value, axis, [(i, i ^ bit) for i in range(count)])


def mm(left, right, dims, out=f32):
    return lax.dot_general(left, right, (dims, ((), ())), preferred_element_type=out)


def gather_pieces(shard):
    rows = shard.shape[0]
    half = rows // 2
    from_x = exchange(shard, "dp", 1)
    from_y = exchange(shard, "dp", 2)
    far_low = exchange(from_x[:half], "dp", 2)
    far_high = exchange(from_y[half:], "dp", 1)
    return [(0, 0, shard), (1, 0, from_x), (2, 0, from_y), (3, 0, far_low), (3, half, far_high)]


def gather_rows(shard, place):
    count = lax.axis_size("dp")
    if count != 4:
        return lax.all_gather(shard, "dp", axis=0, tiled=True)
    rows = shard.shape[0]
    full = jnp.zeros((count * rows, shard.shape[1]), shard.dtype)
    for rel, offset, block in gather_pieces(shard):
        full = lax.dynamic_update_slice(full, block, ((place ^ rel) * rows + offset, 0))
    return full


def gather_rows_shared(shard, place, core):
    count = lax.axis_size("dp")
    if count != 4:
        return lax.all_gather(shard, "dp", axis=0, tiled=True)
    rows, cols = shard.shape
    part = rows // 2
    mine = lax.dynamic_slice(shard, (core * part, 0), (part, cols))
    full = jnp.zeros((count * rows, cols), shard.dtype)
    full = lax.dynamic_update_slice(full, shard, (place * rows, 0))
    for rel, offset, block in gather_pieces(mine)[1:]:
        base = (place ^ rel) * rows + offset
        full = lax.dynamic_update_slice(full, block, (base + core * part, 0))
        full = lax.dynamic_update_slice(
            full, exchange(block, "ctx", 1), (base + (1 - core) * part, 0)
        )
    return full


def scatter_blocks(block_of):
    far = block_of(3, bf16)
    half = far.shape[0] // 2
    low_in = exchange(far[:half], "dp", 1)
    high_in = exchange(far[half:], "dp", 2)
    x_block = block_of(1, f32)
    y_block = block_of(2, f32)
    x_out = jnp.concatenate(
        [x_block[:half].astype(bf16), (x_block[half:] + high_in.astype(f32)).astype(bf16)]
    )
    y_out = jnp.concatenate(
        [(y_block[:half] + low_in.astype(f32)).astype(bf16), y_block[half:].astype(bf16)]
    )
    x_in = exchange(x_out, "dp", 1)
    y_in = exchange(y_out, "dp", 2)
    return block_of(0, f32) + (x_in.astype(f32) + y_in.astype(f32))


def rope_rows(u, cosines, sines):
    return u * cosines + pltpu.roll(u, HEAD_DIM // 2, 1) * sines


def unrope_rows(w, cosines, sines):
    return w * cosines - pltpu.roll(w, HEAD_DIM // 2, 1) * sines


NT = ((1,), (1,))
NN = ((1,), (0,))
TN = ((0,), (0,))


def attend_kernel(q_ref, kv_ref, qcos, qsin, kcos, ksin, qidx, kidx, o_ref, lse_ref, qr_ref, kr_ref, v_ref):
    rows = q_ref.shape[0]
    for g in range(KV_HEADS):
        cols = pl.ds(g * HEAD_DIM, HEAD_DIM)
        kr_ref[:, cols] = rope_rows(kv_ref[:, cols], kcos[...], ksin[...]).astype(bf16)
        v_ref[:, cols] = kv_ref[:, pl.ds(KW + g * HEAD_DIM, HEAD_DIM)].astype(bf16)
    for h in range(HEADS):
        cols = pl.ds(h * HEAD_DIM, HEAD_DIM)
        qr_ref[:, cols] = rope_rows(q_ref[:, cols], qcos[...], qsin[...]).astype(bf16)
    lane = lax.broadcasted_iota(jnp.int32, (rows, HEAD_DIM), 1)
    lse_ref[...] = jnp.zeros_like(lse_ref)

    def step(i, carry):
        g = i * STEP_HEADS // GROUPS
        kcols = pl.ds(pl.multiple_of(g * HEAD_DIM, HEAD_DIM), HEAD_DIM)
        k = kr_ref[:, kcols]
        v = v_ref[:, kcols]
        allowed = kidx[...] <= qidx[...]
        for j in range(STEP_HEADS):
            h = i * STEP_HEADS + j
            cols = pl.ds(pl.multiple_of(h * HEAD_DIM, HEAD_DIM), HEAD_DIM)
            s = mm(qr_ref[:, cols], k, NT) * score_scale
            s = jnp.where(allowed, s, masked_score)
            top = jnp.max(s, axis=-1, keepdims=True)
            e = jnp.exp(s - top)
            total = jnp.sum(e, axis=-1, keepdims=True)
            o = mm(e.astype(bf16), v, NN) / total
            o_ref[:, cols] = o.astype(bf16)
            lse_ref[...] = jnp.where(lane == h, top + jnp.log(total), lse_ref[...])
        return carry

    lax.fori_loop(0, HEADS // STEP_HEADS, step, 0)


def attend_back_kernel(q_ref, k_ref, v_ref, do_ref, lse_ref, qcos, qsin, qidx, kidx, dq_ref, dk_ref, dv_ref):
    rows = q_ref.shape[0]
    lane = lax.broadcasted_iota(jnp.int32, (rows, HEAD_DIM), 1)
    dk_ref[...] = jnp.zeros_like(dk_ref)
    dv_ref[...] = jnp.zeros_like(dv_ref)

    def step(i, carry):
        g = i * STEP_HEADS // GROUPS
        kcols = pl.ds(pl.multiple_of(g * HEAD_DIM, HEAD_DIM), HEAD_DIM)
        k = k_ref[:, kcols]
        v = v_ref[:, kcols]
        allowed = kidx[...] <= qidx[...]
        dk = dk_ref[:, kcols]
        dv = dv_ref[:, kcols]
        for j in range(STEP_HEADS):
            h = i * STEP_HEADS + j
            cols = pl.ds(pl.multiple_of(h * HEAD_DIM, HEAD_DIM), HEAD_DIM)
            q = q_ref[:, cols]
            do = do_ref[:, cols]
            lse = jnp.sum(jnp.where(lane == h, lse_ref[...], 0.0), axis=-1, keepdims=True)
            s = mm(q, k, NT) * score_scale
            p = jnp.where(allowed, jnp.exp(s - lse), 0.0)
            dp = mm(do, v, NT)
            delta = jnp.sum(p * dp, axis=-1, keepdims=True)
            ds = (p * (dp - delta)).astype(bf16)
            dq = mm(ds, k, NN) * score_scale
            dq_ref[:, cols] = unrope_rows(dq, qcos[...], qsin[...]).astype(bf16)
            dk = dk + mm(ds, q, TN) * score_scale
            dv = dv + mm(p.astype(bf16), do, TN)
        dk_ref[:, kcols] = dk
        dv_ref[:, kcols] = dv
        return carry

    lax.fori_loop(0, HEADS // STEP_HEADS, step, 0)


def whole(count):
    return [pl.BlockSpec(memory_space=pltpu.VMEM)] * count


def attend(q_raw, kv_raw, tables_q, tables_k, qidx, kidx):
    rows, keys = q_raw.shape[0], kv_raw.shape[0]
    shape = jax.ShapeDtypeStruct
    return pl.pallas_call(
        attend_kernel,
        out_shape=(
            shape((rows, QW), bf16),
            shape((rows, HEAD_DIM), f32),
            shape((rows, QW), bf16),
            shape((keys, KW), bf16),
            shape((keys, KW), bf16),
        ),
        in_specs=whole(8),
        out_specs=tuple(whole(5)),
        cost_estimate=pl.CostEstimate(
            flops=4 * rows * keys * QW, bytes_accessed=8 * keys * KW, transcendentals=rows * keys * HEADS
        ),
        name="attend",
    )(q_raw, kv_raw, *tables_q, *tables_k, qidx, kidx)


def attend_back(q, k, v, do, lse, tables_q, qidx, kidx):
    rows, keys = q.shape[0], k.shape[0]
    shape = jax.ShapeDtypeStruct
    return pl.pallas_call(
        attend_back_kernel,
        out_shape=(shape((rows, QW), bf16), shape((keys, KW), f32), shape((keys, KW), f32)),
        in_specs=whole(9),
        out_specs=tuple(whole(3)),
        cost_estimate=pl.CostEstimate(
            flops=10 * rows * keys * QW, bytes_accessed=16 * keys * KW, transcendentals=rows * keys * HEADS
        ),
        name="attend_back",
    )(q, k, v, do, lse, *tables_q, qidx, kidx)


def rope_tables(positions):
    half = HEAD_DIM // 2
    steps = jnp.arange(half, dtype=f32)
    frequency = jnp.exp(-math.log(rope_base) * (2.0 * steps / HEAD_DIM))
    angles = positions.astype(f32)[:, None] * frequency[None, :]
    c, s = jnp.cos(angles), jnp.sin(angles)
    return jnp.concatenate([c, c], axis=-1), jnp.concatenate([-s, s], axis=-1)


def unrope(w, cosines, sines):
    heads = w.reshape(w.shape[0], -1, HEAD_DIM)
    rolled = jnp.roll(heads, HEAD_DIM // 2, axis=-1)
    return (heads * cosines[:, None, :] - rolled * sines[:, None, :]).reshape(w.shape)


def inv_rms(rows):
    return lax.rsqrt(jnp.mean(rows * rows, axis=-1, keepdims=True) + norm_eps)


def norm_back(grad_out, normed, inverse, gain):
    scaled = grad_out * gain
    return inverse * (scaled - normed * jnp.mean(scaled * normed, axis=-1, keepdims=True))


def body(
    tokens, positions, block_order, cotangent, gain_attn, w_qkv, b_qkv, w_out, gain_mlp, w_gate, w_up, w_down
):
    _, rows, width = tokens.shape
    n_dp, n_ctx = lax.axis_size("dp"), lax.axis_size("ctx")
    place, ctx = lax.axis_index("dp"), lax.axis_index("ctx")
    core = ctx % 2
    n_all = n_dp * n_ctx
    length = rows * n_ctx
    ff = w_gate.shape[1]
    chunk = ff // n_all
    sub = rows // 2
    proj = QW + 2 * KW

    small = jnp.concatenate([gain_attn, gain_mlp, b_qkv])[None]
    small = lax.all_gather(small, "dp", axis=0, tiled=True)
    d_loc = gain_attn.shape[0]
    gain_one = small[:, :d_loc].reshape(1, width).astype(f32)
    gain_two = small[:, d_loc : 2 * d_loc].reshape(1, width).astype(f32)
    bias = small[:, 2 * d_loc :].reshape(1, proj).astype(f32)

    qkv_full = gather_rows_shared(w_qkv, place, core)
    out_full = gather_rows_shared(w_out, place, core)

    def ff_columns(w):
        return jnp.concatenate(
            [lax.dynamic_slice(w, (0, (d * n_ctx + ctx) * chunk), (w.shape[0], chunk)) for d in range(n_dp)],
            axis=1,
        )

    down = gather_rows(lax.dynamic_slice(w_down, (ctx * chunk, 0), (chunk, width)), place)
    gate = gather_rows(ff_columns(w_gate), place)
    up = gather_rows(ff_columns(w_up), place)

    places = jnp.arange(length, dtype=jnp.int32)
    index = jnp.repeat(block_order, sub) * sub + places % sub
    own_index = lax.dynamic_slice(index, (ctx * rows,), (rows,))
    offset = positions[0, 0] - own_index[0]
    tables_k = rope_tables(index + offset)
    tables_q = tuple(lax.dynamic_slice(t, (ctx * rows, 0), (rows, HEAD_DIM)) for t in tables_k)
    qidx, kidx = own_index[:, None], index[None, :]

    x_full = lax.all_gather(tokens[0], "ctx", axis=0, tiled=True)
    dy_full = lax.all_gather(cotangent[0], "ctx", axis=0, tiled=True)
    x_all = x_full.astype(f32)
    h1_full = (x_all * inv_rms(x_all) * gain_one).astype(bf16)
    x = tokens[0].astype(f32)
    inv1 = inv_rms(x)
    n1 = x * inv1
    h1 = (n1 * gain_one).astype(bf16)
    q_raw = mm(h1, qkv_full[:, :QW], NN) + bias[:, :QW]
    kv_raw = mm(h1_full, qkv_full[:, QW:], NN) + bias[:, QW:]
    ob, lse, q_rot, k_rot, v_rows = attend(q_raw, kv_raw, tables_q, tables_k, qidx, kidx)
    ob_full = lax.all_gather(ob, "ctx", axis=0, tiled=True)
    r1_all = x_all + mm(ob_full, out_full, NN)
    h2_full = (r1_all * inv_rms(r1_all) * gain_two).astype(bf16)
    r1 = lax.dynamic_slice(r1_all, (ctx * rows, 0), (rows, width))
    inv2 = inv_rms(r1)
    n2 = r1 * inv2

    g = mm(h2_full, gate, NN)
    u = mm(h2_full, up, NN)
    sig = jax.nn.sigmoid(g)
    act = (g * sig * u).astype(bf16)
    da = mm(dy_full, down, NT)
    dgate = (da * u * sig * (1.0 + g * (1.0 - sig))).astype(bf16)
    dup = (da * g * sig).astype(bf16)
    dh2_part = (mm(dgate, gate, NT) + mm(dup, up, NT)).astype(bf16)
    dh2 = lax.psum_scatter(dh2_part, "ctx", scatter_dimension=0, tiled=True).astype(f32)
    mlp_part = mm(act, down, NN).astype(bf16)
    mlp = lax.psum_scatter(mlp_part, "ctx", scatter_dimension=0, tiled=True).astype(f32)
    block_out = (r1 + mlp).astype(bf16)[None]

    if n_dp == 4:
        grad_down_all = mm(act, dy_full, TN)

        def down_block(rel, dtype):
            start = (place ^ rel) * chunk
            return lax.dynamic_slice(grad_down_all, (start, 0), (chunk, width)).astype(dtype)

        grad_down = scatter_blocks(down_block)

        def rows_block(grad):
            def block(rel, dtype):
                cols = lax.dynamic_slice(h2_full, (0, (place ^ rel) * d_loc), (length, d_loc))
                return mm(cols, grad, TN, f32).astype(dtype)

            return scatter_blocks(block).astype(bf16)

        gate_rows = rows_block(dgate)
        up_rows = rows_block(dup)
    else:
        scatter = functools.partial(lax.psum_scatter, axis_name="dp", scatter_dimension=0, tiled=True)
        grad_down = scatter(mm(act, dy_full, TN).astype(bf16)).astype(f32)
        gate_rows = scatter(mm(h2_full, dgate, TN).astype(bf16))
        up_rows = scatter(mm(h2_full, dup, TN).astype(bf16))
    own_rows = d_loc // n_ctx
    both = jnp.stack([gate_rows, up_rows]).reshape(2, n_ctx, own_rows, n_dp * chunk).transpose(1, 0, 2, 3)
    both = lax.all_to_all(both, "ctx", 0, 0, tiled=True)

    def natural(part):
        cols = part.reshape(n_ctx, own_rows, n_dp, chunk).transpose(1, 2, 0, 3)
        return cols.reshape(own_rows, ff).astype(f32)

    grad_gate, grad_up = natural(both[:, 0]), natural(both[:, 1])

    grad_gain_two = jnp.sum(dh2 * n2, axis=0)
    dr1 = cotangent[0].astype(f32) + norm_back(dh2, n2, inv2, gain_two)
    dattn = dr1.astype(bf16)
    do = mm(dattn, out_full, NT).astype(bf16)
    dq, dk_part, dv_part = attend_back(q_rot, k_rot, v_rows, do, lse, tables_q, qidx, kidx)
    dkv_part = jnp.concatenate([dk_part, dv_part], axis=1).astype(bf16)
    dkv = lax.psum_scatter(dkv_part, "ctx", scatter_dimension=0, tiled=True).astype(f32)
    dk = unrope(dkv[:, :KW], *tables_q)
    dqkv = jnp.concatenate([dq, dk.astype(bf16), dkv[:, KW:].astype(bf16)], axis=1)
    dh1 = mm(dqkv, qkv_full, NT)
    grad_gain_one = jnp.sum(dh1 * n1, axis=0)
    grad_tokens = (dr1 + norm_back(dh1, n1, inv1, gain_one))[None]
    grad_bias = jnp.sum(dqkv.astype(f32), axis=0)

    def columns(v):
        cols = v.shape[1] // n_ctx
        return lax.all_to_all(v.reshape(rows, n_ctx, cols).transpose(1, 0, 2), "ctx", 0, 0, tiled=True).reshape(length, cols)

    grad_qkv_cols = mm(h1_full, columns(dqkv), TN)
    grad_out_cols = mm(ob_full, columns(dattn), TN)
    cols_qkv, cols_out = proj // n_ctx, width // n_ctx
    share = jnp.concatenate([grad_qkv_cols, grad_out_cols], axis=1).astype(bf16)
    share = share.reshape(n_all, width // n_all, cols_qkv + cols_out)
    share = lax.all_to_all(share, ("dp", "ctx"), 0, 0, tiled=True)
    share = jnp.sum(share.reshape(n_dp, n_ctx, width // n_all, -1).astype(f32), axis=0).transpose(1, 0, 2)
    grad_qkv = share[:, :, :cols_qkv].reshape(width // n_all, proj)
    grad_out = share[:, :, cols_qkv:].reshape(width // n_all, width)
    gain_width = width // n_all
    vectors = jnp.concatenate(
        [grad_gain_one.reshape(n_all, -1), grad_gain_two.reshape(n_all, -1), grad_bias.reshape(n_all, -1)], axis=1
    )
    vectors = jnp.sum(lax.all_to_all(vectors, ("dp", "ctx"), 0, 0, tiled=True), axis=0)
    return (
        block_out,
        grad_tokens,
        vectors[:gain_width],
        grad_qkv,
        vectors[2 * gain_width :],
        grad_out,
        vectors[gain_width : 2 * gain_width],
        grad_gate,
        grad_up,
        grad_down,
    )


def solution(mesh):
    rows = P(("dp", "ctx"), None)
    vector = P(("dp", "ctx"))
    return jax.shard_map(
        body,
        mesh=mesh,
        in_specs=(
            P("dp", "ctx", None),
            P("dp", "ctx"),
            P(),
            P("dp", "ctx", None),
            P("dp"),
            P("dp", None),
            P("dp"),
            P("dp", None),
            P("dp"),
            P("dp", None),
            P("dp", None),
            P("dp", None),
        ),
        out_specs=(
            P("dp", "ctx", None),
            P("dp", "ctx", None),
            vector,
            rows,
            vector,
            rows,
            vector,
            rows,
            rows,
            rows,
        ),
        check_vma=False,
    )
```
